32 devices in a mesh: row: 8 (over y, x, core), col: 4 (over z).
Axes of the slice: x: 2, y: 2, z: 4, core: 2. Of those that a mesh axis runs over, the one named last changes fastest.
Arguments:
- tokens: bfloat16 [48, 8192], P('row'), may hold values from -6 to 6
- cotangent: bfloat16 [48, 8192], P('row'), may hold values from -6 to 6
- gate_weight: bfloat16 [8192, 27648], P('row', 'col'), may hold values from -0.0625 to 0.0625
- up_weight: bfloat16 [8192, 27648], P('row', 'col'), may hold values from -0.0625 to 0.0625
- down_weight: bfloat16 [27648, 8192], P('col', 'row'), may hold values from -0.0390625 to 0.0390625
Outputs:
- output: bfloat16 [48, 8192], P('row')
- grad_tokens: bfloat16 [48, 8192], P('row')
- grad_gate_weight: bfloat16 [8192, 27648], P('row', 'col')
- grad_up_weight: bfloat16 [8192, 27648], P('row', 'col')
- grad_down_weight: bfloat16 [27648, 8192], P('col', 'row')
The draws below stay inside these ranges and needn't reach their ends.
All inputs are finite; a program needn't handle non-finite values.
Results may differ from the reference program's by a relative error of at most 0.0049.
Values may be sent and summed in bfloat16 or wider, within the bound.
A program may use at most 192 MiB of HBM per device.

```python
import jax
import jax.numpy as jnp
from jax import lax

D = 8192
FF = 27648
TOKENS = 48


def block_scale(rng, extent, pieces, smallest, top_value):
    def one(axis_at, parts):
        steps = jax.random.uniform(jax.random.fold_in(jax.random.fold_in(rng, 6), axis_at), (parts,), jnp.float32, smallest / len(pieces), top_value / len(pieces))
        return jnp.repeat(jnp.exp(steps), extent[axis_at] // parts).reshape((-1,) + (1,) * (len(extent) - axis_at - 1))

    level = one(*pieces[0])
    for cut in pieces[1:]:
        level = level * one(*cut)
    return level


def bell_draw(own_key, shape, spread, reach, shards=(), dtype=jnp.bfloat16):
    array = jax.random.normal(own_key, shape, jnp.float32) * spread
    if len(shards) > 0:
        array = block_scale(own_key, shape, shards, -0.22, 0.18) * array
    return jnp.clip(array, min=-reach, max=reach).astype(dtype)


def setup_inputs(seed: int = 0) -> dict:
    arg_keys = jax.random.split(jax.random.key(seed), 6)
    tokens = bell_draw(arg_keys[0], (TOKENS, D), 1.0, 6.0, ((0, 8),))
    cotangent = bell_draw(arg_keys[1], (TOKENS, D), 1.0, 6.0, ((0, 8),))
    gate_weight = bell_draw(arg_keys[2], (D, FF), D ** -0.5, 0.0625, ((0, 8), (1, 4)))
    up_weight = bell_draw(arg_keys[3], (D, FF), D ** -0.5, 0.0625, ((0, 8), (1, 4)))
    down_weight = bell_draw(arg_keys[4], (FF, D), FF ** -0.5, 0.0390625, ((0, 4), (1, 8)))
    return dict(tokens=tokens, cotangent=cotangent, gate_weight=gate_weight, up_weight=up_weight, down_weight=down_weight)


def contract_last(left, right):
    return lax.dot_general(left, right, (((1,), (1,)), ((), ())), preferred_element_type=jnp.float32)


def contract_first(left, right):
    return lax.dot_general(left, right, (((0,), (0,)), ((), ())), preferred_element_type=jnp.float32)


def reference(tokens, cotangent, gate_weight, up_weight, down_weight):
    gate_values = jnp.dot(tokens, gate_weight, preferred_element_type=jnp.float32)
    up_values = jnp.dot(tokens, up_weight, preferred_element_type=jnp.float32)
    sigmoid_gate = jax.nn.sigmoid(gate_values)
    hidden = (gate_values * sigmoid_gate * up_values).astype(jnp.bfloat16)
    output = jnp.dot(hidden, down_weight, preferred_element_type=jnp.float32).astype(jnp.bfloat16)
    grad_hidden = contract_last(cotangent, down_weight)
    grad_gate = (grad_hidden * up_values * sigmoid_gate * (1.0 + gate_values * (1.0 - sigmoid_gate))).astype(jnp.bfloat16)
    grad_up = (grad_hidden * gate_values * sigmoid_gate).astype(jnp.bfloat16)
    grad_tokens = (contract_last(grad_gate, gate_weight) + contract_last(grad_up, up_weight)).astype(jnp.bfloat16)
    grad_gate_weight = contract_first(tokens, grad_gate).astype(jnp.bfloat16)
    grad_up_weight = contract_first(tokens, grad_up).astype(jnp.bfloat16)
    grad_down_weight = contract_first(hidden, cotangent).astype(jnp.bfloat16)
    return (output, grad_tokens, grad_gate_weight, grad_up_weight, grad_down_weight)
```

```python
import functools

import jax
import jax.numpy as jnp
from jax import lax
from jax.experimental import pallas as pl
from jax.experimental.pallas import tpu as pltpu
from jax.sharding import PartitionSpec as P

MESH = pl.DeviceIdType.MESH
BF16 = jnp.bfloat16
F32 = jnp.float32
LANES = 128


def exchange_kernel(
    rows,
    cols,
    width,
    last,
    tc_ref,
    gate_hbm,
    up_hbm,
    down_hbm,
    out_ref,
    gt_ref,
    tiles_ref,
    hid_ref,
    gate_w,
    up_w,
    down_w,
    tok_in,
    tok_f32,
    to_sib,
    from_sib,
    own,
    to_chip,
    from_chip,
    hid,
    acc,
    z_keep,
    z_to,
    z_from,
    r_to,
    fin,
    w_sem,
    tok_s,
    tok_r,
    sib_s,
    sib_r,
    chip_s,
    chip_r,
    ag_s,
    ag_r,
    fwd_s,
    fwd_r,
    zs_s,
    zs_r,
    a2_s,
    a2_r,
    zg_s,
    zg_r,
):
    me = lax.axis_index("row")
    z = lax.axis_index("col")
    chips = rows // 2
    core = lax.rem(me, 2)
    chip = me // 2
    sibling = chip * 2 + (1 - core)
    local = tc_ref.shape[1]
    depth = gate_hbm.shape[0]
    share = depth // cols

    def weight_copies(o, amount):
        start = pl.multiple_of(o * width, LANES)
        return (
            pltpu.make_async_copy(
                gate_hbm.at[:, pl.ds(start, amount)],
                gate_w.at[o, :, pl.ds(0, amount)],
                w_sem.at[0, o],
            ),
            pltpu.make_async_copy(
                up_hbm.at[:, pl.ds(start, amount)],
                up_w.at[o, :, pl.ds(0, amount)],
                w_sem.at[1, o],
            ),
            pltpu.make_async_copy(
                down_hbm.at[pl.ds(start, amount), :],
                down_w.at[o, pl.ds(0, amount), :],
                w_sem.at[2, o],
            ),
        )

    def each_weight(o, act):
        @pl.when(o < rows - 1)
        def _():
            for copy in weight_copies(o, width):
                act(copy)

        @pl.when(o == rows - 1)
        def _():
            for copy in weight_copies(rows - 1, last):
                act(copy)

    for s in range(1, chips + 1):
        k = lax.rem(chip + s, chips)
        each_weight((1 - core) * chips + k, lambda copy: copy.start())
        each_weight(core * chips + k, lambda copy: copy.start())

    barrier = pltpu.get_barrier_semaphore()
    for d in range(1, rows):
        pl.semaphore_signal(
            barrier, inc=1, device_id={"row": lax.rem(me + d, rows), "col": z}, device_id_type=MESH
        )
    for d in range(1, cols):
        pl.semaphore_signal(
            barrier, inc=1, device_id={"row": me, "col": lax.rem(z + d, cols)}, device_id_type=MESH
        )
    pl.semaphore_wait(barrier, rows + cols - 2)

    def remote(src, dst, send, recv, row, col):
        return pltpu.make_async_remote_copy(
            src_ref=src,
            dst_ref=dst,
            send_sem=send,
            recv_sem=recv,
            device_id={"row": row, "col": col},
            device_id_type=MESH,
        )

    tok_copies = []
    for d in range(1, rows):
        peer = lax.rem(me + d, rows)
        columns = pl.ds(pl.multiple_of(peer * depth, LANES), depth)
        copy = remote(
            tc_ref.at[:, :, columns], tok_in.at[me], tok_s.at[d], tok_r.at[d], peer, z
        )
        copy.start()
        tok_copies.append(copy)
    tok_in[me] = tc_ref[:, :, pl.ds(pl.multiple_of(me * depth, LANES), depth)]
    if last < width:
        gate_w[rows - 1, :, last:] = jnp.zeros((depth, width - last), BF16)
        up_w[rows - 1, :, last:] = jnp.zeros((depth, width - last), BF16)
        down_w[rows - 1, last:, :] = jnp.zeros((width - last, depth), BF16)
    acc[...] = jnp.zeros_like(acc)
    for copy in tok_copies:
        copy.wait()
    for r in range(rows):
        for a in range(2):
            tok_f32[a, r * local : (r + 1) * local, :] = tok_in[r, a].astype(F32)
    tiles_ref[...] = tok_f32[...].astype(BF16)

    def partials(o, ref):
        each_weight(o, lambda copy: copy.wait())
        ref[0] = jnp.dot(tiles_ref[0], gate_w[o], preferred_element_type=F32)
        ref[1] = jnp.dot(tiles_ref[0], up_w[o], preferred_element_type=F32)
        ref[2] = lax.dot_general(
            tiles_ref[1], down_w[o], (((1,), (1,)), ((), ())), preferred_element_type=F32
        )

    def sib_copy(s):
        return remote(to_sib.at[s], from_sib.at[s], sib_s.at[s], sib_r.at[s], sibling, z)

    def chip_copy(s):
        peer = lax.rem(chip + s + 1, chips) * 2 + core
        return remote(to_chip.at[s], from_chip.at[s], chip_s.at[s], chip_r.at[s], peer, z)

    def first(s, carry):
        k = lax.rem(chip + s + 1, chips)
        partials((1 - core) * chips + k, to_sib.at[s])
        sib_copy(s).start()
        partials(core * chips + k, own)
        sib_copy(s).wait_recv()
        own[...] = own[...] + from_sib[s]

        @pl.when(s < chips - 1)
        def _():
            to_chip[s] = own[...].astype(BF16)
            chip_copy(s).start()

        return carry

    lax.fori_loop(0, chips, first, 0)

    for s in range(chips - 1):
        chip_copy(s).wait_recv()
    total = own[...]
    for s in range(chips - 1):
        total = total + from_chip[s].astype(F32)
    gate, up, grad_hidden = total[0], total[1], total[2]
    sig = 1.0 / (1.0 + jnp.exp(-gate))
    mine = core * chips + chip
    hid[mine, 0] = (gate * sig * up).astype(BF16)
    hid[mine, 1] = (grad_hidden * up * sig * (1.0 + gate * (1.0 - sig))).astype(BF16)
    hid[mine, 2] = (grad_hidden * gate * sig).astype(BF16)

    def ag_copy(d):
        peer = lax.rem(chip + d, chips) * 2 + core
        return remote(hid.at[mine], hid.at[mine], ag_s.at[d], ag_r.at[d], peer, z)

    def fwd_copy(t):
        o = core * chips + lax.rem(chip + chips - t, chips)
        return remote(hid.at[o], hid.at[o], fwd_s.at[t], fwd_r.at[t], sibling, z)

    for d in range(1, chips):
        ag_copy(d).start()

    def products(o):
        hid_ref[o] = hid[o]
        acc[0] += jnp.dot(hid[o, 0], down_w[o], preferred_element_type=F32)
        acc[1] += lax.dot_general(
            hid[o, 1], gate_w[o], (((1,), (1,)), ((), ())), preferred_element_type=F32
        ) + lax.dot_general(
            hid[o, 2], up_w[o], (((1,), (1,)), ((), ())), preferred_element_type=F32
        )

    def second(t, carry):
        k = lax.rem(chip + chips - t, chips)

        @pl.when(t > 0)
        def _():
            ag_copy(t).wait_recv()

        fwd_copy(t).start()
        products(core * chips + k)
        fwd_copy(t).wait_recv()
        products((1 - core) * chips + k)
        return carry

    lax.fori_loop(0, chips, second, 0)

    for q in range(cols):
        piece = acc[:, :, q * share : (q + 1) * share]
        z_keep[q] = piece
        z_to[q] = piece.astype(BF16)
    z_copies = []
    for d in range(1, cols):
        peer = lax.rem(z + d, cols)
        copy = remote(z_to.at[peer], z_from.at[d], zs_s.at[d], zs_r.at[d], me, peer)
        copy.start()
        z_copies.append(copy)
    summed = z_keep[z]
    for d, copy in enumerate(z_copies):
        copy.wait_recv()
        summed = summed + z_from[d + 1].astype(F32)
    for r in range(rows):
        r_to[r] = summed[:, r * local : (r + 1) * local, :].astype(BF16)
    r_copies = []
    for d in range(1, rows):
        peer = lax.rem(me + d, rows)
        copy = remote(r_to.at[peer], fin.at[z, me], a2_s.at[d], a2_r.at[d], peer, z)
        copy.start()
        r_copies.append(copy)
    fin[z, me] = r_to[me]
    for copy in r_copies:
        copy.wait_recv()
    g_copies = []
    for d in range(1, cols):
        peer = lax.rem(z + d, cols)
        copy = remote(fin.at[z], fin.at[z], zg_s.at[d], zg_r.at[d], me, peer)
        copy.start()
        g_copies.append(copy)
    for copy in g_copies:
        copy.wait_recv()
    for q in range(cols):
        for r in range(rows):
            where = slice(r * depth + q * share, r * depth + (q + 1) * share)
            out_ref[:, where] = fin[q, r, 0]
            gt_ref[:, where] = fin[q, r, 1]

    for copy in z_copies + r_copies + g_copies:
        copy.wait_send()
    for s in range(chips):
        sib_copy(s).wait_send()
        fwd_copy(s).wait_send()
    for s in range(chips - 1):
        chip_copy(s).wait_send()
        ag_copy(s + 1).wait_send()


def weight_grad_kernel(tiles_ref, hid_ref, gate_ref, up_ref, down_ref):
    first = (((0,), (0,)), ((), ()))
    gate_ref[...] = lax.dot_general(
        tiles_ref[0], hid_ref[0, 1], first, preferred_element_type=F32
    ).astype(BF16)
    up_ref[...] = lax.dot_general(
        tiles_ref[0], hid_ref[0, 2], first, preferred_element_type=F32
    ).astype(BF16)
    down_ref[...] = lax.dot_general(
        hid_ref[0, 0], tiles_ref[1], first, preferred_element_type=F32
    ).astype(BF16)


def chunk_width(hidden, rows):
    return -(-hidden // (LANES * rows)) * LANES


def per_device_kernels(rows, cols, tokens, cotangent, gate_weight, up_weight, down_weight):
    local, features = tokens.shape
    depth, hidden = gate_weight.shape
    width = chunk_width(hidden, rows)
    last = hidden - (rows - 1) * width
    count = rows * local
    chips = rows // 2
    share = depth // cols
    both = jnp.stack([tokens, cotangent])
    vmem = pl.BlockSpec(memory_space=pltpu.VMEM)
    hbm = pl.BlockSpec(memory_space=pl.ANY)
    dma = pltpu.SemaphoreType.DMA
    output, grad_tokens, tiles, hid = pl.pallas_call(
        functools.partial(exchange_kernel, rows, cols, width, last),
        out_shape=(
            jax.ShapeDtypeStruct((local, features), BF16),
            jax.ShapeDtypeStruct((local, features), BF16),
            jax.ShapeDtypeStruct((2, count, depth), BF16),
            jax.ShapeDtypeStruct((rows, 3, count, width), BF16),
        ),
        in_specs=[vmem, hbm, hbm, hbm],
        out_specs=(vmem, vmem, vmem, vmem),
        scratch_shapes=[
            pltpu.VMEM((rows, depth, width), BF16),
            pltpu.VMEM((rows, depth, width), BF16),
            pltpu.VMEM((rows, width, depth), BF16),
            pltpu.VMEM((rows, 2, local, depth), BF16),
            pltpu.VMEM((2, count, depth), F32),
            pltpu.VMEM((chips, 3, count, width), F32),
            pltpu.VMEM((chips, 3, count, width), F32),
            pltpu.VMEM((3, count, width), F32),
            pltpu.VMEM((chips - 1, 3, count, width), BF16),
            pltpu.VMEM((chips - 1, 3, count, width), BF16),
            pltpu.VMEM((rows, 3, count, width), BF16),
            pltpu.VMEM((2, count, depth), F32),
            pltpu.VMEM((cols, 2, count, share), F32),
            pltpu.VMEM((cols, 2, count, share), BF16),
            pltpu.VMEM((cols, 2, count, share), BF16),
            pltpu.VMEM((rows, 2, local, share), BF16),
            pltpu.VMEM((cols, rows, 2, local, share), BF16),
            dma((3, rows)),
            dma((rows,)),
            dma((rows,)),
            dma((chips,)),
            dma((chips,)),
            dma((chips,)),
            dma((chips,)),
            dma((chips,)),
            dma((chips,)),
            dma((chips,)),
            dma((chips,)),
            dma((cols,)),
            dma((cols,)),
            dma((rows,)),
            dma((rows,)),
            dma((cols,)),
            dma((cols,)),
        ],
        compiler_params=pltpu.CompilerParams(
            collective_id=0, has_side_effects=True, vmem_limit_bytes=63 * 2**20
        ),
        name="exchange",
    )(both, gate_weight, up_weight, down_weight)
    grads = pl.pallas_call(
        weight_grad_kernel,
        grid=(rows,),
        out_shape=(
            jax.ShapeDtypeStruct((depth, hidden), BF16),
            jax.ShapeDtypeStruct((depth, hidden), BF16),
            jax.ShapeDtypeStruct((hidden, depth), BF16),
        ),
        in_specs=[
            pl.BlockSpec((2, count, depth), lambda i: (0, 0, 0)),
            pl.BlockSpec((1, 3, count, width), lambda i: (i, 0, 0, 0)),
        ],
        out_specs=(
            pl.BlockSpec((depth, width), lambda i: (0, i)),
            pl.BlockSpec((depth, width), lambda i: (0, i)),
            pl.BlockSpec((width, depth), lambda i: (i, 0)),
        ),
        compiler_params=pltpu.CompilerParams(
            dimension_semantics=("arbitrary",), vmem_limit_bytes=40 * 2**20
        ),
        name="weight_grads",
    )(tiles, hid)
    return (output, grad_tokens) + tuple(grads)


def contract_last(left, right):
    return lax.dot_general(
        left, right, (((1,), (1,)), ((), ())), preferred_element_type=jnp.float32
    )


def contract_first(left, right):
    return lax.dot_general(
        left, right, (((0,), (0,)), ((), ())), preferred_element_type=jnp.float32
    )


def row_share(term_fn, local_rows):
    return lax.psum_scatter(
        term_fn(jnp.int32(0), lax.axis_size("row") * local_rows),
        "row",
        scatter_dimension=0,
        tiled=True,
    )


def gather_rows(stacked):
    return lax.all_gather(stacked, "row", axis=1, tiled=True)


def finish(stacked):
    summed = lax.psum(stacked, "col")
    return lax.all_to_all(
        summed.astype(jnp.bfloat16), "row", split_axis=1, concat_axis=2, tiled=True
    )


def hidden_grads(grad_hidden, gate_values, up_values, sigmoid_gate):
    grad_gate = (
        grad_hidden * up_values * sigmoid_gate * (1.0 + gate_values * (1.0 - sigmoid_gate))
    ).astype(jnp.bfloat16)
    grad_up = (grad_hidden * gate_values * sigmoid_gate).astype(jnp.bfloat16)
    return (grad_gate, grad_up)


def activate(gate_values, up_values):
    sigmoid_gate = jax.nn.sigmoid(gate_values)
    hidden = (gate_values * sigmoid_gate * up_values).astype(jnp.bfloat16)
    return (sigmoid_gate, hidden)


def token_grad_term(grad_gate, grad_up, gate_weight, up_weight):
    return contract_last(grad_gate, gate_weight) + contract_last(grad_up, up_weight)


def per_device(tokens, cotangent, gate_weight, up_weight, down_weight):
    tok_tile, cot_tile = (
        lax.all_to_all(tokens, "row", split_axis=1, concat_axis=0, tiled=True),
        lax.all_to_all(cotangent, "row", split_axis=1, concat_axis=0, tiled=True),
    )
    local_rows = tokens.shape[0]
    hidden_width = gate_weight.shape[1]
    both_weights = jnp.concatenate([gate_weight, up_weight], axis=1)

    def forward_term(offset, amount):
        return jnp.dot(tok_tile, both_weights, preferred_element_type=jnp.float32)

    def backward_term(offset, amount):
        return contract_last(cot_tile, down_weight)

    combined = row_share(forward_term, local_rows)
    gate_values = combined[:, :hidden_width]
    up_values = combined[:, hidden_width:]
    sigmoid_gate, hidden_share = activate(gate_values, up_values)
    hidden = gather_rows(hidden_share[None])[0]
    output = finish(jnp.dot(hidden, down_weight, preferred_element_type=jnp.float32)[None])[0]
    grad_hidden = row_share(backward_term, local_rows)
    grad_gate_share, grad_up_share = hidden_grads(grad_hidden, gate_values, up_values, sigmoid_gate)
    gathered = gather_rows(jnp.stack([grad_gate_share, grad_up_share]))
    grad_gate = gathered[0]
    grad_up = gathered[1]
    grad_tokens = finish(token_grad_term(grad_gate, grad_up, gate_weight, up_weight)[None])[0]
    grad_gate_weight = contract_first(tok_tile, grad_gate).astype(jnp.bfloat16)
    grad_up_weight = contract_first(tok_tile, grad_up).astype(jnp.bfloat16)
    grad_down_weight = contract_first(hidden, cot_tile).astype(jnp.bfloat16)
    return (output, grad_tokens, grad_gate_weight, grad_up_weight, grad_down_weight)


VMEM_BUDGET = 60 * 2**20


def fits(rows, cols, local, depth, hidden):
    width = chunk_width(hidden, rows)
    weights = 6 * rows * width * depth
    values = rows * local * width * (36 * rows // 2 + 12 * rows + 12)
    return (
        rows % 2 == 0
        and (rows - 1) * width < hidden
        and depth % (cols * LANES) == 0
        and weights + values < VMEM_BUDGET
    )


def solution(mesh):
    rows, cols = mesh.shape["row"], mesh.shape["col"]

    def per_device_any(tokens, cotangent, gate_weight, up_weight, down_weight):
        depth, hidden = gate_weight.shape
        args = (tokens, cotangent, gate_weight, up_weight, down_weight)
        if fits(rows, cols, tokens.shape[0], depth, hidden):
            return per_device_kernels(rows, cols, *args)
        return per_device(*args)

    return jax.shard_map(
        per_device_any,
        mesh=mesh,
        in_specs=(
            P("row", None),
            P("row", None),
            P("row", "col"),
            P("row", "col"),
            P("col", "row"),
        ),
        out_specs=(
            P("row", None),
            P("row", None),
            P("row", "col"),
            P("row", "col"),
            P("col", "row"),
        ),
        check_vma=False,
    )
```

```python
import functools

import jax
import jax.numpy as jnp
from jax import lax
from jax.experimental import pallas as pl
from jax.experimental.pallas import tpu as pltpu
from jax.sharding import PartitionSpec as P

MESH = pl.DeviceIdType.MESH
BF16 = jnp.bfloat16
F32 = jnp.float32
LANES = 128


def exchange_kernel(
    rows,
    cols,
    width,
    last,
    tok_ref,
    cot_ref,
    gate_hbm,
    up_hbm,
    down_hbm,
    out_ref,
    gt_ref,
    tiles_ref,
    hid_ref,
    gate_w,
    up_w,
    down_w,
    tc_ref,
    tok_in,
    tok_f32,
    to_sib,
    from_sib,
    own,
    to_chip,
    from_chip,
    hid,
    acc,
    z_keep,
    z_to,
    z_from,
    r_to,
    fin,
    w_sem,
    tok_s,
    tok_r,
    sib_s,
    sib_r,
    chip_s,
    chip_r,
    ag_s,
    ag_r,
    fwd_s,
    fwd_r,
    zs_s,
    zs_r,
    a2_s,
    a2_r,
    zg_s,
    zg_r,
):
    me = lax.axis_index("row")
    z = lax.axis_index("col")
    chips = rows // 2
    core = lax.rem(me, 2)
    chip = me // 2
    sibling = chip * 2 + (1 - core)
    local = tc_ref.shape[1]
    depth = gate_hbm.shape[0]
    share = depth // cols

    def other(d):
        if chips in (2, 4):
            high = lax.rem(lax.div(chip, 2) + lax.div(d, 2), 2)
            return high * 2 + lax.rem(chip + d, 2)
        return lax.rem(chip + d, chips)

    def source(d):
        if chips in (2, 4):
            return other(d)
        return lax.rem(chip + chips - d, chips)

    def weight_copies(o, amount):
        start = pl.multiple_of(o * width, LANES)
        return (
            pltpu.make_async_copy(
                gate_hbm.at[:, pl.ds(start, amount)],
                gate_w.at[o, :, pl.ds(0, amount)],
                w_sem.at[0, o],
            ),
            pltpu.make_async_copy(
                up_hbm.at[:, pl.ds(start, amount)],
                up_w.at[o, :, pl.ds(0, amount)],
                w_sem.at[1, o],
            ),
            pltpu.make_async_copy(
                down_hbm.at[pl.ds(start, amount), :],
                down_w.at[o, pl.ds(0, amount), :],
                w_sem.at[2, o],
            ),
        )

    def each_weight(o, act):
        @pl.when(o < rows - 1)
        def _():
            for copy in weight_copies(o, width):
                act(copy)

        @pl.when(o == rows - 1)
        def _():
            for copy in weight_copies(rows - 1, last):
                act(copy)

    for s in range(chips):
        k = other(jnp.int32(chips - 1 - s))
        each_weight((1 - core) * chips + k, lambda copy: copy.start())
        each_weight(core * chips + k, lambda copy: copy.start())

    barrier = pltpu.get_barrier_semaphore()
    for d in range(1, rows):
        pl.semaphore_signal(
            barrier, inc=1, device_id={"row": lax.rem(me + d, rows), "col": z}, device_id_type=MESH
        )
    for d in range(1, cols):
        pl.semaphore_signal(
            barrier, inc=1, device_id={"row": me, "col": lax.rem(z + d, cols)}, device_id_type=MESH
        )
    pl.semaphore_wait(barrier, rows + cols - 2)

    def remote(src, dst, send, recv, row, col):
        return pltpu.make_async_remote_copy(
            src_ref=src,
            dst_ref=dst,
            send_sem=send,
            recv_sem=recv,
            device_id={"row": row, "col": col},
            device_id_type=MESH,
        )

    tc_ref[0] = tok_ref[...]
    tc_ref[1] = cot_ref[...]
    tok_copies = []
    for d in range(1, rows):
        peer = lax.rem(me + d, rows)
        columns = pl.ds(pl.multiple_of(peer * depth, LANES), depth)
        copy = remote(
            tc_ref.at[:, :, columns], tok_in.at[me], tok_s.at[d], tok_r.at[d], peer, z
        )
        copy.start()
        tok_copies.append(copy)
    tok_in[me] = tc_ref[:, :, pl.ds(pl.multiple_of(me * depth, LANES), depth)]
    if last < width:
        gate_w[rows - 1, :, last:] = jnp.zeros((depth, width - last), BF16)
        up_w[rows - 1, :, last:] = jnp.zeros((depth, width - last), BF16)
        down_w[rows - 1, last:, :] = jnp.zeros((width - last, depth), BF16)
    acc[...] = jnp.zeros_like(acc)
    for copy in tok_copies:
        copy.wait_recv()
    for r in range(rows):
        for a in range(2):
            tok_f32[a, r * local : (r + 1) * local, :] = tok_in[r, a].astype(F32)
    tiles_ref[...] = tok_f32[...].astype(BF16)

    def partials(o, ref, ready):
        each_weight(o, lambda copy: copy.wait())
        ref[0] = jnp.dot(tiles_ref[0], gate_w[o], preferred_element_type=F32)
        ready(0)
        ref[1] = jnp.dot(tiles_ref[0], up_w[o], preferred_element_type=F32)
        ready(1)
        ref[2] = lax.dot_general(
            tiles_ref[1], down_w[o], (((1,), (1,)), ((), ())), preferred_element_type=F32
        )
        ready(2)

    def sib_copy(s, a):
        return remote(
            to_sib.at[s, a], from_sib.at[s, a], sib_s.at[s, a], sib_r.at[s, a], sibling, z
        )

    def chip_copy(s, a):
        peer = other(chips - 1 - s) * 2 + core
        return remote(
            to_chip.at[s, a], from_chip.at[s, a], chip_s.at[s, a], chip_r.at[s, a], peer, z
        )

    def first(s, carry):
        k = other(chips - 1 - s)
        partials((1 - core) * chips + k, to_sib.at[s], lambda a: sib_copy(s, a).start())
        partials(core * chips + k, own, lambda a: None)
        for a in range(3):
            sib_copy(s, a).wait_recv()
            value = own[a] + from_sib[s, a]
            own[a] = value

            @pl.when(s < chips - 1)
            def _():
                to_chip[s, a] = value.astype(BF16)
                chip_copy(s, a).start()

        return carry

    lax.fori_loop(0, chips, first, 0)

    for s in range(chips - 1):
        for a in range(3):
            chip_copy(jnp.int32(s), a).wait_recv()
    total = own[...]
    for s in range(chips - 1):
        total = total + from_chip[s].astype(F32)
    gate, up, grad_hidden = total[0], total[1], total[2]
    sig = 1.0 / (1.0 + jnp.exp(-gate))
    mine = core * chips + chip

    def ag_copy(a, d):
        peer = other(d) * 2 + core
        piece = hid.at[mine, a]
        return remote(piece, piece, ag_s.at[a, d], ag_r.at[a, d], peer, z)

    def fwd_copy(a, t):
        piece = hid.at[core * chips + source(t), a]
        return remote(piece, piece, fwd_s.at[a, t], fwd_r.at[a, t], sibling, z)

    hid[mine, 0] = (gate * sig * up).astype(BF16)
    for d in range(1, chips):
        ag_copy(0, jnp.int32(d)).start()
    hid[mine, 1] = (grad_hidden * up * sig * (1.0 + gate * (1.0 - sig))).astype(BF16)
    hid[mine, 2] = (grad_hidden * gate * sig).astype(BF16)

    def product(a, o):
        value = hid[o, a]
        hid_ref[o, a] = value
        if a == 0:
            acc[0] += jnp.dot(value, down_w[o], preferred_element_type=F32)
        else:
            acc[1] += lax.dot_general(
                value,
                (gate_w, up_w)[a - 1][o],
                (((1,), (1,)), ((), ())),
                preferred_element_type=F32,
            )

    def gather_multiply(a, midway):
        def body(t, carry):
            k = source(t)

            @pl.when(t > 0)
            def _():
                ag_copy(a, t).wait_recv()
                if a < 2:
                    ag_copy(a + 1, t).start()

            fwd_copy(a, t).start()
            product(a, core * chips + k)

            if midway is not None:
                pl.when(t == 1)(midway)
            fwd_copy(a, t).wait_recv()
            product(a, (1 - core) * chips + k)
            return carry

        lax.fori_loop(0, chips, body, 0)

    def z_copy(a, d):
        peer = lax.rem(z + d, cols)
        return remote(z_to.at[a, peer], z_from.at[a, d], zs_s.at[a, d], zs_r.at[a, d], me, peer)

    def r_copy(a, d):
        peer = lax.rem(me + d, rows)
        return remote(r_to.at[a, peer], fin.at[a, z, me], a2_s.at[a, d], a2_r.at[a, d], peer, z)

    def g_copy(a, d):
        peer = lax.rem(z + d, cols)
        return remote(fin.at[a, z], fin.at[a, z], zg_s.at[a, d], zg_r.at[a, d], me, peer)

    def start_sum(a):
        for q in range(cols):
            piece = acc[a, :, q * share : (q + 1) * share]
            z_keep[a, q] = piece
            z_to[a, q] = piece.astype(BF16)
        for d in range(1, cols):
            z_copy(a, d).start()

    def start_swap(a):
        summed = z_keep[a, z]
        for d in range(1, cols):
            z_copy(a, d).wait_recv()
            summed = summed + z_from[a, d].astype(F32)
        for r in range(rows):
            r_to[a, r] = summed[r * local : (r + 1) * local, :].astype(BF16)
        for d in range(1, rows):
            r_copy(a, d).start()
        fin[a, z, me] = r_to[a, me]

    def start_spread(a):
        for d in range(1, rows):
            r_copy(a, d).wait_recv()
        for d in range(1, cols):
            g_copy(a, d).start()

    def write_out(a, ref):
        for d in range(1, cols):
            g_copy(a, d).wait_recv()
        for q in range(cols):
            for r in range(rows):
                ref[:, r * depth + q * share : r * depth + (q + 1) * share] = fin[a, q, r]

    gather_multiply(0, None)
    start_sum(0)
    gather_multiply(1, functools.partial(start_swap, 0))
    gather_multiply(2, functools.partial(start_spread, 0))
    start_sum(1)
    write_out(0, out_ref)
    start_swap(1)
    start_spread(1)
    write_out(1, gt_ref)

    for a in range(2):
        for d in range(1, cols):
            z_copy(a, d).wait_send()
            g_copy(a, d).wait_send()
        for d in range(1, rows):
            r_copy(a, d).wait_send()
    for copy in tok_copies:
        copy.wait_send()
    for s in range(chips):
        for a in range(3):
            sib_copy(s, a).wait_send()
            fwd_copy(a, jnp.int32(s)).wait_send()
    for s in range(chips - 1):
        for a in range(3):
            chip_copy(jnp.int32(s), a).wait_send()
            ag_copy(a, jnp.int32(s + 1)).wait_send()


ROWS_AT_ONCE = 128


def weight_grad_kernel(
    tiles_ref, hid_ref, out_in, gt_in, gate_ref, up_ref, down_ref, out_ref, gt_ref, tok_t, hid_t
):
    @pl.when(pl.program_id(0) == 0)
    def _():
        out_ref[...] = out_in[...]
        gt_ref[...] = gt_in[...]
        tok_t[...] = tiles_ref[0].T

    hid_t[...] = hid_ref[0, 0].T
    for start in range(0, tok_t.shape[0], ROWS_AT_ONCE):
        block = slice(start, start + ROWS_AT_ONCE)
        left = tok_t[block, :]
        gate_ref[block, :] = jnp.dot(
            left, hid_ref[0, 1], preferred_element_type=F32
        ).astype(BF16)
        up_ref[block, :] = jnp.dot(left, hid_ref[0, 2], preferred_element_type=F32).astype(BF16)
    for start in range(0, hid_t.shape[0], ROWS_AT_ONCE):
        block = slice(start, start + ROWS_AT_ONCE)
        down_ref[block, :] = jnp.dot(
            hid_t[block, :], tiles_ref[1], preferred_element_type=F32
        ).astype(BF16)


def chunk_width(hidden, rows):
    return -(-hidden // (LANES * rows)) * LANES


def per_device_kernels(rows, cols, tokens, cotangent, gate_weight, up_weight, down_weight):
    local, features = tokens.shape
    depth, hidden = gate_weight.shape
    width = chunk_width(hidden, rows)
    last = hidden - (rows - 1) * width
    count = rows * local
    chips = rows // 2
    share = depth // cols
    vmem = pl.BlockSpec(memory_space=pltpu.VMEM)
    hbm = pl.BlockSpec(memory_space=pl.ANY)
    dma = pltpu.SemaphoreType.DMA
    output, grad_tokens, tiles, hid = pl.pallas_call(
        functools.partial(exchange_kernel, rows, cols, width, last),
        out_shape=(
            jax.ShapeDtypeStruct((local, features), BF16),
            jax.ShapeDtypeStruct((local, features), BF16),
            jax.ShapeDtypeStruct((2, count, depth), BF16),
            jax.ShapeDtypeStruct((rows, 3, count, width), BF16),
        ),
        in_specs=[vmem, vmem, hbm, hbm, hbm],
        out_specs=(vmem, vmem, vmem, vmem),
        scratch_shapes=[
            pltpu.VMEM((rows, depth, width), BF16),
            pltpu.VMEM((rows, depth, width), BF16),
            pltpu.VMEM((rows, width, depth), BF16),
            pltpu.VMEM((2, local, features), BF16),
            pltpu.VMEM((rows, 2, local, depth), BF16),
            pltpu.VMEM((2, count, depth), F32),
            pltpu.VMEM((chips, 3, count, width), F32),
            pltpu.VMEM((chips, 3, count, width), F32),
            pltpu.VMEM((3, count, width), F32),
            pltpu.VMEM((chips - 1, 3, count, width), BF16),
            pltpu.VMEM((chips - 1, 3, count, width), BF16),
            pltpu.VMEM((rows, 3, count, width), BF16),
            pltpu.VMEM((2, count, depth), F32),
            pltpu.VMEM((2, cols, count, share), F32),
            pltpu.VMEM((2, cols, count, share), BF16),
            pltpu.VMEM((2, cols, count, share), BF16),
            pltpu.VMEM((2, rows, local, share), BF16),
            pltpu.VMEM((2, cols, rows, local, share), BF16),
            dma((3, rows)),
            dma((rows,)),
            dma((rows,)),
            dma((chips, 3)),
            dma((chips, 3)),
            dma((chips, 3)),
            dma((chips, 3)),
            dma((3, chips)),
            dma((3, chips)),
            dma((3, chips)),
            dma((3, chips)),
            dma((2, cols)),
            dma((2, cols)),
            dma((2, rows)),
            dma((2, rows)),
            dma((2, cols)),
            dma((2, cols)),
        ],
        compiler_params=pltpu.CompilerParams(
            collective_id=0, has_side_effects=True, vmem_limit_bytes=63 * 2**20
        ),
        name="exchange",
    )(tokens, cotangent, gate_weight, up_weight, down_weight)
    gate_grad, up_grad, down_grad, output, grad_tokens = pl.pallas_call(
        weight_grad_kernel,
        grid=(rows,),
        out_shape=(
            jax.ShapeDtypeStruct((depth, hidden), BF16),
            jax.ShapeDtypeStruct((depth, hidden), BF16),
            jax.ShapeDtypeStruct((hidden, depth), BF16),
            jax.ShapeDtypeStruct((local, features), BF16),
            jax.ShapeDtypeStruct((local, features), BF16),
        ),
        in_specs=[
            pl.BlockSpec((2, count, depth), lambda i: (0, 0, 0)),
            pl.BlockSpec((1, 3, count, width), lambda i: (i, 0, 0, 0)),
            pl.BlockSpec((local, features), lambda i: (0, 0)),
            pl.BlockSpec((local, features), lambda i: (0, 0)),
        ],
        out_specs=(
            pl.BlockSpec((depth, width), lambda i: (0, i)),
            pl.BlockSpec((depth, width), lambda i: (0, i)),
            pl.BlockSpec((width, depth), lambda i: (i, 0)),
            pl.BlockSpec((local, features), lambda i: (0, 0)),
            pl.BlockSpec((local, features), lambda i: (0, 0)),
        ),
        scratch_shapes=[pltpu.VMEM((depth, count), BF16), pltpu.VMEM((width, count), BF16)],
        compiler_params=pltpu.CompilerParams(
            dimension_semantics=("arbitrary",), vmem_limit_bytes=62 * 2**20
        ),
        name="weight_grads",
    )(tiles, hid, output, grad_tokens)
    return (output, grad_tokens, gate_grad, up_grad, down_grad)


def contract_last(left, right):
    return lax.dot_general(
        left, right, (((1,), (1,)), ((), ())), preferred_element_type=jnp.float32
    )


def contract_first(left, right):
    return lax.dot_general(
        left, right, (((0,), (0,)), ((), ())), preferred_element_type=jnp.float32
    )


def row_share(term_fn, local_rows):
    return lax.psum_scatter(
        term_fn(jnp.int32(0), lax.axis_size("row") * local_rows),
        "row",
        scatter_dimension=0,
        tiled=True,
    )


def gather_rows(stacked):
    return lax.all_gather(stacked, "row", axis=1, tiled=True)


def finish(stacked):
    summed = lax.psum(stacked, "col")
    return lax.all_to_all(
        summed.astype(jnp.bfloat16), "row", split_axis=1, concat_axis=2, tiled=True
    )


def hidden_grads(grad_hidden, gate_values, up_values, sigmoid_gate):
    grad_gate = (
        grad_hidden * up_values * sigmoid_gate * (1.0 + gate_values * (1.0 - sigmoid_gate))
    ).astype(jnp.bfloat16)
    grad_up = (grad_hidden * gate_values * sigmoid_gate).astype(jnp.bfloat16)
    return (grad_gate, grad_up)


def activate(gate_values, up_values):
    sigmoid_gate = jax.nn.sigmoid(gate_values)
    hidden = (gate_values * sigmoid_gate * up_values).astype(jnp.bfloat16)
    return (sigmoid_gate, hidden)


def token_grad_term(grad_gate, grad_up, gate_weight, up_weight):
    return contract_last(grad_gate, gate_weight) + contract_last(grad_up, up_weight)


def per_device(tokens, cotangent, gate_weight, up_weight, down_weight):
    tok_tile, cot_tile = (
        lax.all_to_all(tokens, "row", split_axis=1, concat_axis=0, tiled=True),
        lax.all_to_all(cotangent, "row", split_axis=1, concat_axis=0, tiled=True),
    )
    local_rows = tokens.shape[0]
    hidden_width = gate_weight.shape[1]
    both_weights = jnp.concatenate([gate_weight, up_weight], axis=1)

    def forward_term(offset, amount):
        return jnp.dot(tok_tile, both_weights, preferred_element_type=jnp.float32)

    def backward_term(offset, amount):
        return contract_last(cot_tile, down_weight)

    combined = row_share(forward_term, local_rows)
    gate_values = combined[:, :hidden_width]
    up_values = combined[:, hidden_width:]
    sigmoid_gate, hidden_share = activate(gate_values, up_values)
    hidden = gather_rows(hidden_share[None])[0]
    output = finish(jnp.dot(hidden, down_weight, preferred_element_type=jnp.float32)[None])[0]
    grad_hidden = row_share(backward_term, local_rows)
    grad_gate_share, grad_up_share = hidden_grads(grad_hidden, gate_values, up_values, sigmoid_gate)
    gathered = gather_rows(jnp.stack([grad_gate_share, grad_up_share]))
    grad_gate = gathered[0]
    grad_up = gathered[1]
    grad_tokens = finish(token_grad_term(grad_gate, grad_up, gate_weight, up_weight)[None])[0]
    grad_gate_weight = contract_first(tok_tile, grad_gate).astype(jnp.bfloat16)
    grad_up_weight = contract_first(tok_tile, grad_up).astype(jnp.bfloat16)
    grad_down_weight = contract_first(hidden, cot_tile).astype(jnp.bfloat16)
    return (output, grad_tokens, grad_gate_weight, grad_up_weight, grad_down_weight)


VMEM_BUDGET = 60 * 2**20


def fits(rows, cols, local, depth, hidden):
    width = chunk_width(hidden, rows)
    weights = 6 * rows * width * depth
    values = rows * local * width * (36 * rows // 2 + 12 * rows + 12)
    return (
        rows % 2 == 0
        and (rows - 1) * width < hidden
        and depth % (cols * LANES) == 0
        and weights + values < VMEM_BUDGET
    )


def solution(mesh):
    rows, cols = mesh.shape["row"], mesh.shape["col"]

    def per_device_any(tokens, cotangent, gate_weight, up_weight, down_weight):
        depth, hidden = gate_weight.shape
        args = (tokens, cotangent, gate_weight, up_weight, down_weight)
        if fits(rows, cols, tokens.shape[0], depth, hidden):
            return per_device_kernels(rows, cols, *args)
        return per_device(*args)

    return jax.shard_map(
        per_device_any,
        mesh=mesh,
        in_specs=(
            P("row", None),
            P("row", None),
            P("row", "col"),
            P("row", "col"),
            P("col", "row"),
        ),
        out_specs=(
            P("row", None),
            P("row", None),
            P("row", "col"),
            P("row", "col"),
            P("col", "row"),
        ),
        check_vma=False,
    )
```
